128 devices in a mesh: grp: 8 (over y, core), row: 16 (over z, x).
Axes of the slice: x: 4, y: 4, z: 4, core: 2. Of those that a mesh axis runs over, the one named last changes fastest.
Arguments:
- grad: float32 [128, 2048, 512], P('grp', 'row')
- weight: bfloat16 [128, 2048, 512], P('grp', 'row'), may hold values from -0.125 to 0.125
- owner: int32 [128, 1], P('grp'), may hold values from 0 to 15; in each aligned block of 16 rows (0 to 15, 16 to 31, ...) at most 2 rows name the same one
- tokens: bfloat16 [6144, 2048], P('row'), may hold values from -6 to 6
- counts: int32 [16], P('row'), may hold values from 96 to 384, as said below
Outputs:
- new_weight: bfloat16 [128, 2048, 512], P('grp', 'row')
- mixed: bfloat16 [6144, 512], P('row', 'grp')
The draws below stay inside these ranges and needn't reach their ends.
Inputs may be any that keep to these rules, and one draw needn't show every extreme that they name: Within each group's 16 consecutive matrices no owner is named more than 2 times, a bound that some block reaches. `counts`: some row index has all 384 rows live.
All inputs are finite; a program needn't handle non-finite values.
Results may differ from the reference program's by a relative error of at most 0.017.
Values may be sent and summed in bfloat16 or wider, within the bound.
No kernel may reach another device: no remote copies, remote signals or barrier semaphores. Data moves between devices by JAX's collectives and lax.ppermute only.
A program may use at most 128 MiB of HBM per device.

```python
import math
import jax
import jax.numpy as jnp
import numpy as np
from jax import lax

H = 2048
F = 512
TOK_DEV = 384
ITERS = 5
MOST = 2
EXP_G = 16
EXPERTS = 128
TOKENS = 6144
N_GRP = 8
N_ROW = 16


def draw_grad(key, part):
    keys = jax.random.split(jax.random.fold_in(key, 11), 3)
    shape = (EXPERTS, H, F)
    base = jax.random.normal(keys[0], shape, jnp.float32)
    row_scale = jnp.exp(jax.random.uniform(keys[1], (EXPERTS, H, 1), jnp.float32) * math.log(10.0))
    rising = jnp.exp(math.log(3.0) * jnp.arange(H, dtype=jnp.float32) / H)[None, :, None]
    col_scale = jnp.exp(jax.random.uniform(keys[2], (EXPERTS, 1, F), jnp.float32) * math.log(10.0))
    return base * row_scale * rising * col_scale


def draw_counts(key, part):
    keys = jax.random.split(jax.random.fold_in(key, 23), 2)
    values = jax.random.randint(keys[0], (N_ROW,), TOK_DEV // 4, TOK_DEV + 1)
    chosen = jax.random.randint(keys[1], (), 0, N_ROW)
    return jnp.where(jnp.arange(N_ROW) == chosen, TOK_DEV, values).astype(jnp.int32)


def block_scale(rng, dims, shards, least, largest):
    gain, own = 1.0, jax.random.fold_in(rng, 6)
    for position, shards_of in shards:
        steps = jnp.exp(jax.random.uniform(jax.random.fold_in(own, position), (shards_of,), jnp.float32, least / len(shards), largest / len(shards)))
        gain = gain * jnp.repeat(steps, dims[position] // shards_of).reshape([-1 if axis == position else 1 for axis in range(len(dims))])
    return gain


def routed_block(rng, own, number, rows, number_of, top, bound, slope):
    order = jax.random.permutation(rng, number_of)
    crowded, usual = portions_of(number_of, rows * top, bound, slope, True), portions_of(number_of, rows * top, bound, slope, False)
    places = jnp.arange(number_of)

    def named(sizes, turn):
        used = int((sizes > 0).sum())
        fixed = max(1, used // 4)
        passed = fixed + (places - fixed + turn * (used - fixed)) % max(1, number_of - fixed)
        return jnp.zeros((number_of,), jnp.int32).at[order[jnp.where(places < fixed, places, passed)]].set(jnp.asarray(sizes, jnp.int32))

    sizes = jnp.where(number % 4 == 0, named(crowded, number // 4), named(usual, number - number // 4 - 1))
    mixed = jax.random.permutation(jax.random.fold_in(own, 3), number_of)
    giver, sink = mixed[0:number_of // 2 * 2:2], mixed[1:number_of // 2 * 2:2]
    slack = jnp.minimum(sizes[giver] - 1, bound - sizes[sink]) // 2
    slack = jnp.where((giver == order[0]) | (sink == order[0]) | (sizes[sink] == 0), 0, jnp.maximum(slack, 0))
    passed = jax.random.randint(jax.random.fold_in(own, 4), (number_of // 2,), 0, 1 << 20) % (slack + 1)
    sizes = sizes.at[giver].add(-passed).at[sink].add(passed)
    labels = jnp.searchsorted(jnp.cumsum(sizes), jnp.arange(rows * top), side="right").astype(jnp.int32)
    grid = labels.reshape(top, rows).T
    grid = grid[jax.random.permutation(jax.random.fold_in(own, 1), rows)]
    turn = jax.random.randint(jax.random.fold_in(own, 2), (rows, 1), 0, top)
    return jnp.take_along_axis(grid, (jnp.arange(top)[None, :] + turn) % top, axis=1)


def portions_of(number_of, total, bound, slope, full):
    loads = [(1 << 20) // math.isqrt(grade ** slope) + 1 for grade in range(1, number_of + 1)]
    largest = bound if full else min(bound, max(-(-total // number_of), total * loads[0] // sum(loads)))
    least = 1 if total - largest >= number_of - 1 else 0
    given, spare = [largest] + [least] * (number_of - 1), total - largest - least * (number_of - 1)
    while spare > 0:
        free = [i for i in range(1, number_of) if given[i] < largest] or [i for i in range(1, number_of) if given[i] < bound]
        pool, left = sum([loads[i] for i in free]), spare
        for i in free:
            extra = min(bound - given[i], max(1, left * loads[i] // pool), spare)
            given[i] = given[i] + extra
            spare = spare - extra
    return np.array(given)


def gaussian(key, dims, spread, reach, shards=(), held_as=jnp.bfloat16):
    result = spread * jax.random.normal(key, dims, jnp.float32)
    if shards:
        result = result * block_scale(key, dims, shards, -0.22, 0.18)
    return jnp.clip(result, -reach, reach).astype(held_as)


def setup_inputs(seed: int = 0) -> dict:
    splits = jax.random.split(jax.random.key(seed), 6)
    grad = draw_grad(jax.random.fold_in(splits[5], 71), 0)
    weight = gaussian(splits[1], (EXPERTS, H, F), H ** -0.5, 0.125, ((0, 8), (1, 16)))
    owner_keys = jax.random.split(jax.random.fold_in(splits[2], 1), EXPERTS // EXP_G)
    owner_turns = jax.random.permutation(jax.random.fold_in(splits[2], 3), EXPERTS // EXP_G)
    owner = jax.vmap(lambda own, number: routed_block(jax.random.fold_in(splits[2], 2), own, number, EXP_G, N_ROW, 1, MOST, 2))(owner_keys, owner_turns).reshape((EXPERTS, 1))
    tokens = gaussian(splits[3], (TOKENS, H), 1.0, 6.0, ((0, 16),))
    counts = draw_counts(jax.random.fold_in(splits[5], 71), 0)
    return {"grad": grad, "weight": weight, "owner": owner, "tokens": tokens, "counts": counts}


coef_a = 3.4445
coef_b = -4.775
coef_c = 2.0315
step_size = 0.5

def newton_schulz(start):
    iterate_state = start
    for turn in range(ITERS):
        gram_product = jnp.dot(iterate_state.T, iterate_state, preferred_element_type=jnp.float32).astype(jnp.bfloat16)
        square = jnp.dot(gram_product, gram_product, preferred_element_type=jnp.float32)
        polynomial_term = (coef_b * gram_product.astype(jnp.float32) + coef_c * square).astype(jnp.bfloat16)
        iterate_state = (coef_a * iterate_state.astype(jnp.float32) + jnp.dot(iterate_state, polynomial_term, preferred_element_type=jnp.float32)).astype(jnp.bfloat16)
    return iterate_state

def reference(grad, weight, owner, tokens, counts):
    norm2 = lax.optimization_barrier(jnp.sum(grad * grad, axis=(1, 2)))
    start = (grad / (jnp.sqrt(norm2) + 1e-07)[:, None, None]).astype(jnp.bfloat16)
    blocks = tokens.reshape(N_ROW, TOK_DEV, H)

    def turn_one(total, item):
        matrix, old, target = item
        ortho = newton_schulz(matrix)
        recent_matrix = (old.astype(jnp.float32) - step_size * ortho.astype(jnp.float32)).astype(jnp.bfloat16)
        rows_in = lax.dynamic_index_in_dim(blocks, target, 0, keepdims=False)
        term = jnp.dot(rows_in, recent_matrix, preferred_element_type=jnp.float32)
        total = total.at[target].add(term)
        return (total, recent_matrix)
    initial_total0 = jnp.zeros((N_ROW, TOK_DEV, F), jnp.float32)
    total, new_weight = lax.scan(turn_one, initial_total0, (start, weight, owner[:, 0].astype(jnp.int32)))
    proj = total * N_GRP ** (-0.5)
    live = jnp.arange(TOK_DEV)[None, :, None] < counts[:, None, None]
    mixed = jnp.where(live, proj, 0.0).reshape(N_ROW * TOK_DEV, F).astype(jnp.bfloat16)
    return (new_weight, mixed)
```

```python
import jax
import jax.numpy as jnp
from jax import lax
from jax.experimental import pallas as pl
from jax.experimental.pallas import tpu as pltpu
from jax.sharding import Mesh
from jax.sharding import PartitionSpec as P

ITERS = 5
coef_a = 3.4445
coef_b = -4.775
coef_c = 2.0315
step_size = 0.5

f32 = jnp.float32
bf16 = jnp.bfloat16


def orthogonalize(x_ref, o_ref):
    rows, width = x_ref.shape
    step = rows // 4
    scale = None
    for turn in range(ITERS):
        source = x_ref if turn == 0 else o_ref
        x = source[...]
        gram = lax.dot_general(x, x, (((0,), (0,)), ((), ())), preferred_element_type=f32)
        if turn == 0:
            diagonal = lax.broadcasted_iota(jnp.int32, gram.shape, 0) == lax.broadcasted_iota(
                jnp.int32, gram.shape, 1
            )
            norm2 = jnp.sum(
                jnp.sum(jnp.where(diagonal, gram, 0.0), axis=0, keepdims=True),
                axis=1,
                keepdims=True,
            )
            scale = 1.0 / (jnp.sqrt(norm2) + 1e-07)
            gram = jnp.where(norm2 < jnp.inf, gram * scale * scale, 0.0)
        g = gram.astype(bf16)
        square = jnp.dot(g, g, preferred_element_type=f32)
        poly = (coef_b * g.astype(f32) + coef_c * square).astype(bf16)
        for part in range(4):
            at = pl.ds(part * step, step)
            piece = source[at, :]
            fresh = coef_a * piece.astype(f32) + jnp.dot(piece, poly, preferred_element_type=f32)
            if turn == 0:
                fresh = fresh * scale
            o_ref[at, :] = fresh.astype(bf16)


def update(owner_ref, core_ref, weight_ref, ortho_ref, new_ref, keep_ref, send_ref, table):
    number, halves, rows, width = weight_ref.shape
    owners = keep_ref.shape[1]
    tiles = width // 128

    @pl.when(pl.program_id(0) == 0)
    def _():
        for r in range(owners):
            table[0, r] = -1
            table[1, r] = -1
        for e in range(number):
            o = owner_ref[e]
            seen = table[0, o] >= 0
            table[1, o] = jnp.where(seen, e, table[1, o])
            table[0, o] = jnp.where(seen, table[0, o], e)

    for e in range(number):
        new_ref[e] = (
            weight_ref[e].astype(f32) - step_size * ortho_ref[e].astype(f32)
        ).astype(bf16)

    low = lax.broadcasted_iota(jnp.int32, (rows, 128), 1) < 64
    first_core = core_ref[0] == 0
    for r in range(owners):
        one, two = table[0, r], table[1, r]
        total = jnp.where(one >= 0, new_ref[jnp.maximum(one, 0)].astype(f32), 0.0)
        total = total + jnp.where(two >= 0, new_ref[jnp.maximum(two, 0)].astype(f32), 0.0)
        for t in range(tiles):
            top = total[0, :, t * 128 : (t + 1) * 128]
            bottom = pltpu.roll(total[1, :, t * 128 : (t + 1) * 128], 64, 1)
            mine = low == first_core
            keep_ref[t, r] = jnp.where(mine, top, bottom).astype(bf16)
            send_ref[t, r] = jnp.where(mine, bottom, top).astype(bf16)


def project(count_ref, core_ref, tokens_ref, sums_ref, out_ref, held):
    planes, owners, rows, lanes = sums_ref.shape
    for r in range(owners):
        total = sums_ref[0, r].astype(f32)
        for y in range(1, planes):
            total = total + sums_ref[y, r].astype(f32)
        held[pl.ds(r * 2 * rows, rows), :] = total.astype(bf16)
        held[pl.ds(r * 2 * rows + rows, rows), :] = pltpu.roll(total, 64, 1).astype(bf16)
    full = jnp.dot(tokens_ref[...], held[...], preferred_element_type=f32)
    mine = jnp.where(core_ref[0] == 0, full, pltpu.roll(full, 64, 1))[:, :64]
    live = lax.broadcasted_iota(jnp.int32, mine.shape, 0) < count_ref[0]
    out_ref[...] = jnp.where(live, mine * 8 ** (-0.5), 0.0).astype(bf16)


def body(grad, weight, owner, tokens, counts):
    number, rows, width = grad.shape
    ranks = lax.axis_size("row")
    planes = lax.axis_size("y")
    core = lax.axis_index("core")[None]
    vmem = pl.BlockSpec(memory_space=pltpu.VMEM)
    smem = pl.BlockSpec(memory_space=pltpu.SMEM)
    params = pltpu.CompilerParams(vmem_limit_bytes=48 * 1024 * 1024)

    whole = lax.all_to_all(grad.astype(bf16), "row", split_axis=0, concat_axis=0, tiled=True)
    ortho = pl.pallas_call(
        orthogonalize,
        out_shape=jax.ShapeDtypeStruct((ranks * rows, width), bf16),
        in_specs=[vmem],
        out_specs=vmem,
        compiler_params=params,
        name="orthogonalize",
    )(whole.reshape(ranks * rows, width))
    back = lax.all_to_all(
        ortho.reshape(ranks, rows, width), "row", split_axis=0, concat_axis=0, tiled=True
    )

    half = rows // 2
    block = pl.BlockSpec((number, 2, 16, width), lambda i: (0, 0, i, 0))
    packed = pl.BlockSpec((planes, ranks, 16, 128), lambda i: (0, 0, i, 0))
    new, keep, send = pl.pallas_call(
        update,
        grid=(half // 16,),
        out_shape=(
            jax.ShapeDtypeStruct((number, 2, half, width), bf16),
            jax.ShapeDtypeStruct((planes, ranks, half, 128), bf16),
            jax.ShapeDtypeStruct((planes, ranks, half, 128), bf16),
        ),
        in_specs=[smem, smem, block, block],
        out_specs=(block, packed, packed),
        scratch_shapes=[pltpu.SMEM((2, ranks), jnp.int32)],
        compiler_params=params,
        name="update",
    )(
        owner[:, 0],
        core,
        weight.reshape(number, 2, half, width),
        back.reshape(number, 2, half, width),
    )
    other = lax.ppermute(send, "core", [(0, 1), (1, 0)])
    pair = (keep.astype(f32) + other.astype(f32)).astype(bf16)
    sums = lax.all_to_all(
        pair.reshape(planes * ranks, half, 128),
        ("y", "row"),
        split_axis=0,
        concat_axis=0,
        tiled=True,
    ).reshape(planes, ranks, half, 128)
    mixed = pl.pallas_call(
        project,
        out_shape=jax.ShapeDtypeStruct((tokens.shape[0], width // (2 * planes)), bf16),
        in_specs=[smem, smem, vmem, vmem],
        out_specs=vmem,
        scratch_shapes=[pltpu.VMEM((ranks * rows, 128), bf16)],
        compiler_params=params,
        name="project",
    )(counts, core, tokens, sums)
    return new.reshape(number, rows, width), mixed


def solution(mesh):
    devices = mesh.devices.reshape(mesh.shape["grp"] // 2, 2, mesh.shape["row"])
    inner = Mesh(devices, ("y", "core", "row"))
    group = ("y", "core")
    return jax.shard_map(
        body,
        mesh=inner,
        in_specs=(
            P(group, "row", None),
            P(group, "row", None),
            P(group, None),
            P("row", None),
            P("row"),
        ),
        out_specs=(P(group, "row", None), P("row", group)),
        check_vma=False,
    )
```

```python
import jax
import jax.numpy as jnp
from jax import lax
from jax.experimental import pallas as pl
from jax.experimental.pallas import tpu as pltpu
from jax.sharding import Mesh
from jax.sharding import PartitionSpec as P

ITERS = 5
coef_a = 3.4445
coef_b = -4.775
coef_c = 2.0315
step_size = 0.5

f32 = jnp.float32
bf16 = jnp.bfloat16


def orthogonalize(x_ref, out_ref, held, staged, sems):
    rows = x_ref.shape[0]
    copies = []
    step = rows // 4
    scale = None
    for turn in range(ITERS):
        source = x_ref if turn == 0 else held
        x = source[...]
        gram = lax.dot_general(x, x, (((0,), (0,)), ((), ())), preferred_element_type=f32)
        if turn == 0:
            diagonal = lax.broadcasted_iota(jnp.int32, gram.shape, 0) == lax.broadcasted_iota(
                jnp.int32, gram.shape, 1
            )
            norm2 = jnp.sum(
                jnp.sum(jnp.where(diagonal, gram, 0.0), axis=0, keepdims=True),
                axis=1,
                keepdims=True,
            )
            scale = 1.0 / (jnp.sqrt(norm2) + 1e-07)
            gram = jnp.where(norm2 < jnp.inf, gram * scale * scale, 0.0)
        g = gram.astype(bf16)
        square = jnp.dot(g, g, preferred_element_type=f32)
        poly = (coef_b * g.astype(f32) + coef_c * square).astype(bf16)
        for part in range(4):
            at = pl.ds(part * step, step)
            piece = source[at, :]
            fresh = coef_a * piece.astype(f32) + jnp.dot(piece, poly, preferred_element_type=f32)
            if turn == 0:
                fresh = fresh * scale
            fresh = fresh.astype(bf16)
            if turn < ITERS - 1:
                held[at, :] = fresh
                continue
            staged[at, :] = fresh
            copies.append(pltpu.make_async_copy(staged.at[at], out_ref.at[at], sems.at[part]))
            copies[-1].start()
    for copy in copies:
        copy.wait()


def combine(owner_ref, pair_ref, core_ref, mine_ref, theirs_ref, ortho_ref, *refs):
    sum_ref, pass_ref, staged, table, sems, pass_sem = refs
    number, halves, rows, width = ortho_ref.shape
    lanes = rows // 2
    tiles = width // 128
    core = core_ref[0]
    passing = pltpu.make_async_copy(ortho_ref.at[:, 1 - core], pass_ref, pass_sem)
    passing.start()
    for source, named in enumerate((owner_ref, pair_ref)):
        for r in range(number):
            table[2 * source, r] = -1
            table[2 * source + 1, r] = -1
        for e in range(number):
            o = named[e]
            seen = table[2 * source, o] >= 0
            table[2 * source + 1, o] = jnp.where(seen, e, table[2 * source + 1, o])
            table[2 * source, o] = jnp.where(seen, table[2 * source, o], e)

    low = lax.broadcasted_iota(jnp.int32, (lanes, 128), 1) < 64
    copies = []
    for r in range(number):
        total = 0.0
        for slot in range(4):
            e = table[slot, r]
            at = jnp.maximum(e, 0)
            old_ref, source = (mine_ref, core) if slot < 2 else (theirs_ref, 1 - core)
            new = old_ref[at].astype(f32) - step_size * ortho_ref[at, source].astype(f32)
            total = total + jnp.where(e >= 0, new, 0.0)
        for t in range(tiles):
            top = total[:lanes, t * 128 : (t + 1) * 128]
            bottom = pltpu.roll(total[lanes:, t * 128 : (t + 1) * 128], 64, 1)
            staged[r, 2 * t] = jnp.where(low, top, bottom).astype(bf16)
            staged[r, 2 * t + 1] = jnp.where(low, bottom, top).astype(bf16)
        if r % 4 == 3:
            ready = pl.ds(r - 3, 4)
            copies.append(
                pltpu.make_async_copy(staged.at[ready], sum_ref.at[ready], sems.at[r // 4])
            )
            copies[-1].start()
    for copy in copies:
        copy.wait()
    passing.wait()


def project(count_ref, core_ref, tokens_ref, sums_ref, out_ref, held):
    ranks, planes, halves, rows, _ = sums_ref.shape
    for r in range(ranks):
        for h in range(halves):
            first = (2 * r + h) * 2 * rows
            total = sums_ref[r, 0, h].astype(f32)
            for y in range(1, planes):
                total = total + sums_ref[r, y, h].astype(f32)
            held[first : first + rows, :] = total.astype(bf16)
            held[first + rows : first + 2 * rows, :] = pltpu.roll(total, 64, 1).astype(bf16)
    full = jnp.dot(tokens_ref[...], held[...], preferred_element_type=f32).T
    mine = jnp.where(core_ref[0] == 0, full[:64], full[64:])
    live = lax.broadcasted_iota(jnp.int32, mine.shape, 1) < count_ref[0]
    out_ref[...] = jnp.where(live, mine * 8 ** (-0.5), 0.0).astype(bf16)


def body(grad, weight, owner, tokens, counts):
    number, rows, width = grad.shape
    ranks = lax.axis_size("row")
    planes = lax.axis_size("y")
    half = rows // 2
    index = lax.axis_index("core")
    core = index[None]
    vmem = pl.BlockSpec(memory_space=pltpu.VMEM)
    smem = pl.BlockSpec(memory_space=pltpu.SMEM)
    hbm = pl.BlockSpec(memory_space=pltpu.HBM)
    params = pltpu.CompilerParams(vmem_limit_bytes=20 * 1024 * 1024)
    swap = [(0, 1), (1, 0)]

    def exchange(data, axes):
        return lax.all_to_all(data, axes, split_axis=0, concat_axis=0, tiled=True)

    whole = exchange(grad.astype(bf16), "row")

    named = owner[:, 0]
    pair_named = lax.ppermute(named, "core", swap)
    split = weight.reshape(number, 2, half, width)
    mine = lax.dynamic_index_in_dim(split, index, 1, keepdims=False)
    theirs = lax.ppermute(
        lax.dynamic_index_in_dim(split, 1 - index, 1, keepdims=False), "core", swap
    )
    ortho = pl.pallas_call(
        orthogonalize,
        out_shape=pltpu.HBM((ranks * rows, width), bf16),
        in_specs=[vmem],
        out_specs=hbm,
        scratch_shapes=[
            pltpu.VMEM((ranks * rows, width), bf16),
            pltpu.VMEM((ranks * rows, width), bf16),
            pltpu.SemaphoreType.DMA((4,)),
        ],
        compiler_params=params,
        name="orthogonalize",
    )(whole.reshape(ranks * rows, width))
    back = exchange(ortho.reshape(2 * ranks, half, width), ("row", "core"))
    back = back.reshape(number, 2, half, width)

    lanes = half // 2
    sums, passed = pl.pallas_call(
        combine,
        out_shape=(
            pltpu.HBM((ranks, 2 * planes, lanes, 128), bf16),
            pltpu.HBM((number, half, width), bf16),
        ),
        in_specs=[smem, smem, smem, vmem, vmem, vmem],
        out_specs=(hbm, hbm),
        scratch_shapes=[
            pltpu.VMEM((ranks, 2 * planes, lanes, 128), bf16),
            pltpu.SMEM((4, number), jnp.int32),
            pltpu.SemaphoreType.DMA((4,)),
            pltpu.SemaphoreType.DMA,
        ],
        compiler_params=params,
        name="combine",
    )(named, pair_named, core, mine, theirs, back)
    sums = exchange(sums.reshape(-1, lanes, 128), ("row", "y", "core"))
    sums = sums.reshape(ranks, planes, 2, lanes, 128)

    other = lax.ppermute(passed, "core", swap)
    own = lax.dynamic_index_in_dim(back, index, 1, keepdims=False)
    move = jnp.concatenate(
        [jnp.where(index == 0, own, other), jnp.where(index == 0, other, own)], axis=1
    )
    new = (weight.astype(f32) - step_size * move.astype(f32)).astype(bf16)
    new, sums = lax.optimization_barrier((new, sums))
    mixed = pl.pallas_call(
        project,
        out_shape=jax.ShapeDtypeStruct((width // (2 * planes), tokens.shape[0]), bf16),
        in_specs=[smem, smem, vmem, vmem],
        out_specs=vmem,
        scratch_shapes=[pltpu.VMEM((ranks * rows, 128), bf16)],
        compiler_params=params,
        name="project",
    )(counts, core, tokens, sums)
    return new, mixed.T


def solution(mesh):
    devices = mesh.devices.reshape(mesh.shape["grp"] // 2, 2, mesh.shape["row"])
    inner = Mesh(devices, ("y", "core", "row"))
    group = ("y", "core")
    return jax.shard_map(
        body,
        mesh=inner,
        in_specs=(
            P(group, "row", None),
            P(group, "row", None),
            P(group, None),
            P("row", None),
            P("row"),
        ),
        out_specs=(P(group, "row", None), P("row", group)),
        check_vma=False,
    )
```

```python
import jax
import jax.numpy as jnp
from jax import lax
from jax.experimental import pallas as pl
from jax.experimental.pallas import tpu as pltpu
from jax.sharding import Mesh
from jax.sharding import PartitionSpec as P

ITERS = 5
coef_a = 3.4445
coef_b = -4.775
coef_c = 2.0315
step_size = 0.5

f32 = jnp.float32
bf16 = jnp.bfloat16


def orthogonalize(x_ref, out_ref, held, staged, sems):
    rows = x_ref.shape[0]
    copies = []
    step = rows // 4
    scale = None
    for turn in range(ITERS):
        source = x_ref if turn == 0 else held
        x = source[...]
        gram = lax.dot_general(x, x, (((0,), (0,)), ((), ())), preferred_element_type=f32)
        if turn == 0:
            diagonal = lax.broadcasted_iota(jnp.int32, gram.shape, 0) == lax.broadcasted_iota(
                jnp.int32, gram.shape, 1
            )
            norm2 = jnp.sum(
                jnp.sum(jnp.where(diagonal, gram, 0.0), axis=0, keepdims=True),
                axis=1,
                keepdims=True,
            )
            scale = 1.0 / (jnp.sqrt(norm2) + 1e-07)
            gram = jnp.where(norm2 < jnp.inf, gram * scale * scale, 0.0)
        g = gram.astype(bf16)
        square = jnp.dot(g, g, preferred_element_type=f32)
        poly = (coef_b * g.astype(f32) + coef_c * square).astype(bf16)
        for part in range(4):
            at = pl.ds(part * step, step)
            piece = source[at, :]
            fresh = coef_a * piece.astype(f32) + jnp.dot(piece, poly, preferred_element_type=f32)
            if turn == 0:
                fresh = fresh * scale
            fresh = fresh.astype(bf16)
            if turn < ITERS - 1:
                held[at, :] = fresh
                continue
            staged[at, :] = fresh
            copies.append(pltpu.make_async_copy(staged.at[at], out_ref.at[at], sems.at[part]))
            copies[-1].start()
    for copy in copies:
        copy.wait()


def list_owned(named, table, base):
    for r in range(named.shape[0]):
        table[base, r] = -1
        table[base + 1, r] = -1
    for e in range(named.shape[0]):
        o = named[e]
        seen = table[base, o] >= 0
        table[base + 1, o] = jnp.where(seen, e, table[base + 1, o])
        table[base, o] = jnp.where(seen, table[base, o], e)


def gather_old(owner_ref, core_ref, weight_ref, keep_ref, send_ref, held, staged, table, *sems):
    in_sems, out_sems = sems
    number, rows, width = weight_ref.shape
    half = rows // 2
    core = core_ref[0]
    arriving = []
    for part in range(4):
        some = pl.ds(part * (number // 4), number // 4)
        arriving.append(
            pltpu.make_async_copy(weight_ref.at[some], held.at[some], in_sems.at[part])
        )
        arriving[-1].start()
    list_owned(owner_ref, table, 0)
    for copy in arriving:
        copy.wait()
    copies = []
    for place, out_ref in enumerate((send_ref, keep_ref)):
        near = core if place else 1 - core
        at = pl.ds(pl.multiple_of(near * half, half), half)
        for r in range(number):
            total = 0.0
            for slot in range(2):
                e = table[slot, r]
                old = held[jnp.maximum(e, 0), at, :].astype(f32)
                total = total + jnp.where(e >= 0, old, 0.0)
            staged[place, r] = total.astype(bf16)
        copies.append(pltpu.make_async_copy(staged.at[place], out_ref, out_sems.at[place]))
        copies[-1].start()
    for copy in copies:
        copy.wait()


def combine(owner_ref, pair_ref, core_ref, mine_ref, theirs_ref, ortho_ref, *refs):
    sum_ref, pass_ref, held, staged, table, in_sems, sems, pass_sem = refs
    number, halves, rows, width = ortho_ref.shape
    lanes = rows // 2
    tiles = width // 128
    core = core_ref[0]
    arriving = []
    for part in range(4):
        some = pl.ds(part * (number // 4), number // 4)
        arriving.append(pltpu.make_async_copy(mine_ref.at[some], held.at[some], in_sems.at[part]))
        arriving[-1].start()
    passing = pltpu.make_async_copy(ortho_ref.at[:, 1 - core], pass_ref, pass_sem)
    passing.start()
    list_owned(owner_ref, table, 0)
    list_owned(pair_ref, table, 2)

    low = lax.broadcasted_iota(jnp.int32, (lanes, 128), 1) < 64
    copies = []
    for r in range(number):
        if r % 4 == 0:
            arriving[r // 4].wait()
        move = 0.0
        for slot in range(4):
            e = table[slot, r]
            source = core if slot < 2 else 1 - core
            one = ortho_ref[jnp.maximum(e, 0), source].astype(f32)
            move = move + jnp.where(e >= 0, one, 0.0)
        total = held[r].astype(f32) + theirs_ref[r].astype(f32) - step_size * move
        for t in range(tiles):
            top = total[:lanes, t * 128 : (t + 1) * 128]
            bottom = pltpu.roll(total[lanes:, t * 128 : (t + 1) * 128], 64, 1)
            staged[r, 2 * t] = jnp.where(low, top, bottom).astype(bf16)
            staged[r, 2 * t + 1] = jnp.where(low, bottom, top).astype(bf16)
        if r % 4 == 3:
            ready = pl.ds(r - 3, 4)
            copies.append(
                pltpu.make_async_copy(staged.at[ready], sum_ref.at[ready], sems.at[r // 4])
            )
            copies[-1].start()
    for copy in copies:
        copy.wait()
    passing.wait()


def project(count_ref, core_ref, tokens_ref, sums_ref, out_ref, held):
    ranks, planes, halves, rows, _ = sums_ref.shape
    for r in range(ranks):
        for h in range(halves):
            first = (2 * r + h) * 2 * rows
            total = sums_ref[r, 0, h].astype(f32)
            for y in range(1, planes):
                total = total + sums_ref[r, y, h].astype(f32)
            held[first : first + rows, :] = total.astype(bf16)
            held[first + rows : first + 2 * rows, :] = pltpu.roll(total, 64, 1).astype(bf16)
    full = jnp.dot(tokens_ref[...], held[...], preferred_element_type=f32).T
    mine = jnp.where(core_ref[0] == 0, full[:64], full[64:])
    live = lax.broadcasted_iota(jnp.int32, mine.shape, 1) < count_ref[0]
    out_ref[...] = jnp.where(live, mine * 8 ** (-0.5), 0.0).astype(bf16)


def body(grad, weight, owner, tokens, counts):
    number, rows, width = grad.shape
    ranks = lax.axis_size("row")
    planes = lax.axis_size("y")
    half = rows // 2
    index = lax.axis_index("core")
    core = index[None]
    vmem = pl.BlockSpec(memory_space=pltpu.VMEM)
    smem = pl.BlockSpec(memory_space=pltpu.SMEM)
    hbm = pl.BlockSpec(memory_space=pltpu.HBM)
    params = pltpu.CompilerParams(vmem_limit_bytes=20 * 1024 * 1024)
    swap = [(0, 1), (1, 0)]

    def exchange(data, axes):
        return lax.all_to_all(data, axes, split_axis=0, concat_axis=0, tiled=True)

    whole = exchange(grad.astype(bf16), "row")

    named = owner[:, 0]
    pair_named = lax.ppermute(named, "core", swap)
    mine, theirs = pl.pallas_call(
        gather_old,
        out_shape=(
            pltpu.HBM((ranks, half, width), bf16),
            pltpu.HBM((ranks, half, width), bf16),
        ),
        in_specs=[smem, smem, hbm],
        out_specs=(hbm, hbm),
        scratch_shapes=[
            pltpu.VMEM((number, rows, width), bf16),
            pltpu.VMEM((2, ranks, half, width), bf16),
            pltpu.SMEM((2, number), jnp.int32),
            pltpu.SemaphoreType.DMA((4,)),
            pltpu.SemaphoreType.DMA((2,)),
        ],
        compiler_params=params,
        name="gather_old",
    )(named, core, pltpu.with_memory_space_constraint(weight, pltpu.HBM))
    theirs = lax.ppermute(theirs, "core", swap)

    ortho = pl.pallas_call(
        orthogonalize,
        out_shape=pltpu.HBM((ranks * rows, width), bf16),
        in_specs=[vmem],
        out_specs=hbm,
        scratch_shapes=[
            pltpu.VMEM((ranks * rows, width), bf16),
            pltpu.VMEM((ranks * rows, width), bf16),
            pltpu.SemaphoreType.DMA((4,)),
        ],
        compiler_params=params,
        name="orthogonalize",
    )(whole.reshape(ranks * rows, width))
    back = exchange(ortho.reshape(2 * ranks, half, width), ("row", "core"))
    back = back.reshape(number, 2, half, width)

    lanes = half // 2
    sums, passed = pl.pallas_call(
        combine,
        out_shape=(
            pltpu.HBM((ranks, 2 * planes, lanes, 128), bf16),
            pltpu.HBM((number, half, width), bf16),
        ),
        in_specs=[smem, smem, smem, hbm, vmem, vmem],
        out_specs=(hbm, hbm),
        scratch_shapes=[
            pltpu.VMEM((ranks, half, width), bf16),
            pltpu.VMEM((ranks, 2 * planes, lanes, 128), bf16),
            pltpu.SMEM((4, number), jnp.int32),
            pltpu.SemaphoreType.DMA((4,)),
            pltpu.SemaphoreType.DMA((4,)),
            pltpu.SemaphoreType.DMA,
        ],
        compiler_params=params,
        name="combine",
    )(
        named,
        pair_named,
        core,
        pltpu.with_memory_space_constraint(mine, pltpu.HBM),
        theirs,
        back,
    )
    sums = exchange(sums.reshape(-1, lanes, 128), ("row", "y", "core"))
    sums = sums.reshape(ranks, planes, 2, lanes, 128)

    other = lax.ppermute(passed, "core", swap)
    own = lax.dynamic_index_in_dim(back, index, 1, keepdims=False)
    move = jnp.concatenate(
        [jnp.where(index == 0, own, other), jnp.where(index == 0, other, own)], axis=1
    )
    new = (weight.astype(f32) - step_size * move.astype(f32)).astype(bf16)
    new, sums = lax.optimization_barrier((new, sums))
    mixed = pl.pallas_call(
        project,
        out_shape=jax.ShapeDtypeStruct((width // (2 * planes), tokens.shape[0]), bf16),
        in_specs=[smem, smem, vmem, vmem],
        out_specs=vmem,
        scratch_shapes=[pltpu.VMEM((ranks * rows, 128), bf16)],
        compiler_params=params,
        name="project",
    )(counts, core, tokens, sums)
    return new, mixed.T


def solution(mesh):
    devices = mesh.devices.reshape(mesh.shape["grp"] // 2, 2, mesh.shape["row"])
    inner = Mesh(devices, ("y", "core", "row"))
    group = ("y", "core")
    return jax.shard_map(
        body,
        mesh=inner,
        in_specs=(
            P(group, "row", None),
            P(group, "row", None),
            P(group, None),
            P("row", None),
            P("row"),
        ),
        out_specs=(P(group, "row", None), P("row", group)),
        check_vma=False,
    )
```

```python
import jax
import jax.numpy as jnp
from jax import lax
from jax.experimental import pallas as pl
from jax.experimental.pallas import tpu as pltpu
from jax.sharding import Mesh
from jax.sharding import PartitionSpec as P

ITERS = 5
coef_a = 3.4445
coef_b = -4.775
coef_c = 2.0315
step_size = 0.5
PIECES = 2

f32 = jnp.float32
bf16 = jnp.bfloat16


def narrow(far_ref, out_ref, held, sems):
    parts = sems.shape[0]
    size = out_ref.shape[0] // parts
    copies = []
    for part in range(parts):
        some = pl.ds(part * size, size)
        copies.append(pltpu.make_async_copy(far_ref.at[some], held.at[some], sems.at[part]))
        copies[-1].start()
    for part in range(parts):
        copies[part].wait()
        some = pl.ds(part * size, size)
        out_ref[some] = held[some].astype(bf16)


def orthogonalize(x_ref, out_ref, held, staged, sems):
    rows = x_ref.shape[0]
    copies = []
    step = rows // 4
    scale = None
    for turn in range(ITERS):
        source = x_ref if turn == 0 else held
        x = source[...]
        gram = lax.dot_general(x, x, (((0,), (0,)), ((), ())), preferred_element_type=f32)
        if turn == 0:
            diagonal = lax.broadcasted_iota(jnp.int32, gram.shape, 0) == lax.broadcasted_iota(
                jnp.int32, gram.shape, 1
            )
            norm2 = jnp.sum(
                jnp.sum(jnp.where(diagonal, gram, 0.0), axis=0, keepdims=True),
                axis=1,
                keepdims=True,
            )
            scale = 1.0 / (jnp.sqrt(norm2) + 1e-07)
            gram = jnp.where(norm2 < jnp.inf, gram * scale * scale, 0.0)
        g = gram.astype(bf16)
        square = jnp.dot(g, g, preferred_element_type=f32)
        poly = (coef_b * g.astype(f32) + coef_c * square).astype(bf16)
        for part in range(4):
            at = pl.ds(part * step, step)
            piece = source[at, :]
            fresh = coef_a * piece.astype(f32) + jnp.dot(piece, poly, preferred_element_type=f32)
            if turn == 0:
                fresh = fresh * scale
            fresh = fresh.astype(bf16)
            if turn < ITERS - 1:
                held[at, :] = fresh
                continue
            staged[at, :] = fresh
            copies.append(pltpu.make_async_copy(staged.at[at], out_ref.at[at], sems.at[part]))
            copies[-1].start()
    for copy in copies:
        copy.wait()


def list_owned(named, table):
    for r in range(named.shape[0]):
        table[0, r] = -1
        table[1, r] = -1
    for e in range(named.shape[0]):
        o = named[e]
        seen = table[0, o] >= 0
        table[1, o] = jnp.where(seen, e, table[1, o])
        table[0, o] = jnp.where(seen, table[0, o], e)


def gather_old(owner_ref, core_ref, weight_ref, keep_ref, send_ref, table, held, staged, *sems):
    in_sems, out_sems = sems
    number, rows, width = weight_ref.shape
    half = rows // 2
    core = core_ref[0]
    arriving = []
    for part in range(4):
        some = pl.ds(part * (number // 4), number // 4)
        arriving.append(
            pltpu.make_async_copy(weight_ref.at[some], held.at[some], in_sems.at[part])
        )
        arriving[-1].start()
    list_owned(owner_ref, table)
    for copy in arriving:
        copy.wait()
    copies = []
    for place, out_ref in enumerate((send_ref, keep_ref)):
        near = core if place else 1 - core
        at = pl.ds(pl.multiple_of(near * half, half), half)
        for r in range(number):
            total = 0.0
            for slot in range(2):
                e = table[slot, r]
                old = held[jnp.maximum(e, 0), at, :].astype(f32)
                total = total + jnp.where(e >= 0, old, 0.0)
            staged[place, r] = total.astype(bf16)
        copies.append(pltpu.make_async_copy(staged.at[place], out_ref, out_sems.at[place]))
        copies[-1].start()
    for copy in copies:
        copy.wait()


def combine(table_ref, pair_ref, core_ref, old_ref, ortho_ref, *refs):
    sum_ref, pass_refs, (staged, sems, pass_sems) = refs[0], refs[1:-3], refs[-3:]
    number, halves, rows, width = ortho_ref.shape
    lanes = rows // 2
    tiles = width // 128
    core = core_ref[0]
    passing = []
    for part, pass_ref in enumerate(pass_refs):
        some = pl.ds(part * pass_ref.shape[0], pass_ref.shape[0])
        passing.append(
            pltpu.make_async_copy(ortho_ref.at[some, 1 - core], pass_ref, pass_sems.at[part])
        )
        passing[-1].start()
    low = lax.broadcasted_iota(jnp.int32, (lanes, 128), 1) < 64
    copies = []
    for r in range(number):
        slots = []
        for slot in range(4):
            e = (table_ref if slot < 2 else pair_ref)[slot % 2, r]
            source = core if slot < 2 else 1 - core
            slots.append((e >= 0, jnp.maximum(e, 0), source))
        for t in range(tiles):
            columns = slice(t * 128, (t + 1) * 128)
            move = 0.0
            for listed, at, source in slots:
                one = ortho_ref[at, source, :, columns].astype(f32)
                move = move + jnp.where(listed, one, 0.0)
            total = old_ref[r, :, columns].astype(f32) - step_size * move
            top = total[:lanes]
            bottom = pltpu.roll(total[lanes:], 64, 1)
            staged[r, 2 * t] = jnp.where(low, top, bottom).astype(bf16)
            staged[r, 2 * t + 1] = jnp.where(low, bottom, top).astype(bf16)
        if r % 2 == 1:
            ready = pl.ds(r - 1, 2)
            copies.append(
                pltpu.make_async_copy(staged.at[ready], sum_ref.at[ready], sems.at[r // 2])
            )
            copies[-1].start()
    for copy in copies:
        copy.wait()
    for copy in passing:
        copy.wait()


def project(count_ref, core_ref, tokens_ref, sums_ref, out_ref, held):
    ranks, planes, halves, rows, _ = sums_ref.shape
    for r in range(ranks):
        for h in range(halves):
            first = (2 * r + h) * 2 * rows
            total = sums_ref[r, 0, h].astype(f32)
            for y in range(1, planes):
                total = total + sums_ref[r, y, h].astype(f32)
            held[first : first + rows, :] = total.astype(bf16)
            held[first + rows : first + 2 * rows, :] = pltpu.roll(total, 64, 1).astype(bf16)
    full = jnp.dot(tokens_ref[...], held[...], preferred_element_type=f32).T
    mine = jnp.where(core_ref[0] == 0, full[:64], full[64:])
    live = lax.broadcasted_iota(jnp.int32, mine.shape, 1) < count_ref[0]
    out_ref[...] = jnp.where(live, mine * 8 ** (-0.5), 0.0).astype(bf16)


def body(grad, weight, owner, tokens, counts):
    number, rows, width = grad.shape
    ranks = lax.axis_size("row")
    planes = lax.axis_size("y")
    half = rows // 2
    index = lax.axis_index("core")
    core = index[None]
    vmem = pl.BlockSpec(memory_space=pltpu.VMEM)
    smem = pl.BlockSpec(memory_space=pltpu.SMEM)
    hbm = pl.BlockSpec(memory_space=pltpu.HBM)
    params = pltpu.CompilerParams(vmem_limit_bytes=20 * 1024 * 1024)
    swap = [(0, 1), (1, 0)]

    def exchange(data, axes):
        return lax.all_to_all(data, axes, split_axis=0, concat_axis=0, tiled=True)

    narrowed = pl.pallas_call(
        narrow,
        out_shape=jax.ShapeDtypeStruct(grad.shape, bf16),
        in_specs=[hbm],
        out_specs=vmem,
        scratch_shapes=[pltpu.VMEM(grad.shape, f32), pltpu.SemaphoreType.DMA((16,))],
        compiler_params=params,
        name="narrow",
    )(pltpu.with_memory_space_constraint(grad, pltpu.HBM))
    whole = exchange(narrowed, "row")

    named = owner[:, 0]
    mine, theirs, table = pl.pallas_call(
        gather_old,
        out_shape=(
            pltpu.HBM((ranks, half, width), bf16),
            pltpu.HBM((ranks, half, width), bf16),
            jax.ShapeDtypeStruct((2, number), jnp.int32),
        ),
        in_specs=[smem, smem, hbm],
        out_specs=(hbm, hbm, smem),
        scratch_shapes=[
            pltpu.VMEM((number, rows, width), bf16),
            pltpu.VMEM((2, ranks, half, width), bf16),
            pltpu.SemaphoreType.DMA((4,)),
            pltpu.SemaphoreType.DMA((2,)),
        ],
        compiler_params=params,
        name="gather_old",
    )(named, core, pltpu.with_memory_space_constraint(weight, pltpu.HBM))
    theirs = lax.ppermute(theirs, "core", swap)
    pair_table = lax.ppermute(table, "core", swap)
    old = (mine.astype(f32) + theirs.astype(f32)).astype(bf16)

    ortho = pl.pallas_call(
        orthogonalize,
        out_shape=pltpu.HBM((ranks * rows, width), bf16),
        in_specs=[vmem],
        out_specs=hbm,
        scratch_shapes=[
            pltpu.VMEM((ranks * rows, width), bf16),
            pltpu.VMEM((ranks * rows, width), bf16),
            pltpu.SemaphoreType.DMA((4,)),
        ],
        compiler_params=params,
        name="orthogonalize",
    )(whole.reshape(ranks * rows, width))
    back = exchange(ortho.reshape(2 * ranks, half, width), ("row", "core"))
    back = back.reshape(number, 2, half, width)

    lanes = half // 2
    sums, *passed = pl.pallas_call(
        combine,
        out_shape=(
            pltpu.HBM((ranks, 2 * planes, lanes, 128), bf16),
            *[pltpu.HBM((number // PIECES, half, width), bf16) for _ in range(PIECES)],
        ),
        in_specs=[smem, smem, smem, vmem, vmem],
        out_specs=(hbm,) * (1 + PIECES),
        scratch_shapes=[
            pltpu.VMEM((ranks, 2 * planes, lanes, 128), bf16),
            pltpu.SemaphoreType.DMA((8,)),
            pltpu.SemaphoreType.DMA((PIECES,)),
        ],
        compiler_params=params,
        name="combine",
    )(
        table,
        pair_table,
        core,
        old,
        back,
    )
    sums = exchange(sums.reshape(-1, lanes, 128), ("row", "y", "core"))
    sums = sums.reshape(ranks, planes, 2, lanes, 128)

    other = jnp.concatenate([lax.ppermute(piece, "core", swap) for piece in passed])
    own = lax.dynamic_index_in_dim(back, index, 1, keepdims=True)
    near = lax.broadcasted_iota(jnp.int32, (1, 2, 1, 1), 1) == index
    move = jnp.where(near, own, other[:, None])
    new = weight.reshape(move.shape).astype(f32) - step_size * move.astype(f32)
    new = new.astype(bf16).reshape(weight.shape)
    new, sums = lax.optimization_barrier((new, sums))
    mixed = pl.pallas_call(
        project,
        out_shape=jax.ShapeDtypeStruct((width // (2 * planes), tokens.shape[0]), bf16),
        in_specs=[smem, smem, vmem, vmem],
        out_specs=vmem,
        scratch_shapes=[pltpu.VMEM((ranks * rows, 128), bf16)],
        compiler_params=params,
        name="project",
    )(counts, core, tokens, sums)
    return new, mixed.T


def solution(mesh):
    devices = mesh.devices.reshape(mesh.shape["grp"] // 2, 2, mesh.shape["row"])
    inner = Mesh(devices, ("y", "core", "row"))
    group = ("y", "core")
    return jax.shard_map(
        body,
        mesh=inner,
        in_specs=(
            P(group, "row", None),
            P(group, "row", None),
            P(group, None),
            P("row", None),
            P("row"),
        ),
        out_specs=(P(group, "row", None), P("row", group)),
        check_vma=False,
    )
```

```python
import jax
import jax.numpy as jnp
from jax import lax
from jax.experimental import pallas as pl
from jax.experimental.pallas import tpu as pltpu
from jax.sharding import Mesh
from jax.sharding import PartitionSpec as P

ITERS = 5
coef_a = 3.4445
coef_b = -4.775
coef_c = 2.0315
step_size = 0.5
PIECES = 2

f32 = jnp.float32
bf16 = jnp.bfloat16


def narrow(far_ref, out_ref, held, sems):
    parts = sems.shape[0]
    size = out_ref.shape[0] // parts
    copies = []
    for part in range(parts):
        some = pl.ds(part * size, size)
        copies.append(pltpu.make_async_copy(far_ref.at[some], held.at[some], sems.at[part]))
        copies[-1].start()
    for part in range(parts):
        copies[part].wait()
        some = pl.ds(part * size, size)
        out_ref[some] = held[some].astype(bf16)


def cross(left, right):
    return lax.dot_general(left, right, (((0,), (0,)), ((), ())), preferred_element_type=f32)


def trace(block):
    diagonal = lax.broadcasted_iota(jnp.int32, block.shape, 0) == lax.broadcasted_iota(
        jnp.int32, block.shape, 1
    )
    total = jnp.sum(jnp.where(diagonal, block, 0.0), axis=0, keepdims=True)
    return jnp.sum(total, axis=1, keepdims=True)


def orthogonalize(x_ref, out_ref, gram_ref, held, staged, sems):
    rows, width = x_ref.shape
    low, high = slice(0, width // 2), slice(width // 2, width)
    copies = []
    scale = None
    for turn in range(ITERS):
        source = x_ref if turn == 0 else held
        left, right = source[:, low], source[:, high]
        upper = cross(left, right)
        if turn == 0:
            first, last = cross(left, left), cross(right, right)
            norm2 = trace(first) + trace(last)
            scale = 1.0 / (jnp.sqrt(norm2) + 1e-07)

            def scaled(block):
                return jnp.where(norm2 < jnp.inf, block * scale * scale, 0.0)

            upper, first, last = scaled(upper), scaled(first), scaled(last)
        gram_ref[low, high] = upper.astype(bf16)
        gram_ref[high, low] = upper.T.astype(bf16)
        gram_ref[low, low] = (first if turn == 0 else cross(left, left)).astype(bf16)
        gram_ref[high, high] = (last if turn == 0 else cross(right, right)).astype(bf16)
        g = gram_ref[...]
        square = jnp.dot(g, g, preferred_element_type=f32)
        poly = (coef_b * g.astype(f32) + coef_c * square).astype(bf16)
        parts = 4 if turn < ITERS - 1 else sems.shape[0]
        step = rows // parts
        for part in range(parts):
            at = pl.ds(part * step, step)
            piece = source[at, :]
            fresh = coef_a * piece.astype(f32) + jnp.dot(piece, poly, preferred_element_type=f32)
            if turn == 0:
                fresh = fresh * scale
            fresh = fresh.astype(bf16)
            if turn < ITERS - 1:
                held[at, :] = fresh
                continue
            staged[at, :] = fresh
            copies.append(pltpu.make_async_copy(staged.at[at], out_ref.at[at], sems.at[part]))
            copies[-1].start()
    for copy in copies:
        copy.wait()


def list_owned(named, table):
    for r in range(named.shape[0]):
        table[0, r] = -1
        table[1, r] = -1
    for e in range(named.shape[0]):
        o = named[e]
        seen = table[0, o] >= 0
        table[1, o] = jnp.where(seen, e, table[1, o])
        table[0, o] = jnp.where(seen, table[0, o], e)


def gather_old(owner_ref, core_ref, weight_ref, keep_ref, send_ref, table, held, staged, *sems):
    in_sems, out_sems = sems
    number, rows, width = weight_ref.shape
    half = rows // 2
    core = core_ref[0]
    arriving = []
    for part in range(4):
        some = pl.ds(part * (number // 4), number // 4)
        arriving.append(
            pltpu.make_async_copy(weight_ref.at[some], held.at[some], in_sems.at[part])
        )
        arriving[-1].start()
    list_owned(owner_ref, table)
    for copy in arriving:
        copy.wait()
    copies = []
    for place, out_ref in enumerate((send_ref, keep_ref)):
        near = core if place else 1 - core
        at = pl.ds(pl.multiple_of(near * half, half), half)
        for r in range(number):
            total = 0.0
            for slot in range(2):
                e = table[slot, r]
                old = held[jnp.maximum(e, 0), at, :].astype(f32)
                total = total + jnp.where(e >= 0, old, 0.0)
            staged[place, r] = total.astype(bf16)
        copies.append(pltpu.make_async_copy(staged.at[place], out_ref, out_sems.at[place]))
        copies[-1].start()
    for copy in copies:
        copy.wait()


def combine(table_ref, pair_ref, core_ref, old_ref, ortho_ref, *refs):
    sum_ref, pass_refs, (staged, sems, pass_sems) = refs[0], refs[1:-3], refs[-3:]
    number, halves, rows, width = ortho_ref.shape
    lanes = rows // 2
    tiles = width // 128
    core = core_ref[0]
    passing = []
    for part, pass_ref in enumerate(pass_refs):
        some = pl.ds(part * pass_ref.shape[0], pass_ref.shape[0])
        passing.append(
            pltpu.make_async_copy(ortho_ref.at[some, 1 - core], pass_ref, pass_sems.at[part])
        )
        passing[-1].start()
    low = lax.broadcasted_iota(jnp.int32, (lanes, 128), 1) < 64
    copies = []
    for r in range(number):
        slots = []
        for slot in range(4):
            e = (table_ref if slot < 2 else pair_ref)[slot % 2, r]
            source = core if slot < 2 else 1 - core
            slots.append((e >= 0, jnp.maximum(e, 0), source))
        for t in range(tiles):
            columns = slice(t * 128, (t + 1) * 128)
            move = 0.0
            for listed, at, source in slots:
                one = ortho_ref[at, source, :, columns].astype(f32)
                move = move + jnp.where(listed, one, 0.0)
            total = old_ref[r, :, columns].astype(f32) - step_size * move
            top = total[:lanes]
            bottom = pltpu.roll(total[lanes:], 64, 1)
            staged[r, 2 * t] = jnp.where(low, top, bottom).astype(bf16)
            staged[r, 2 * t + 1] = jnp.where(low, bottom, top).astype(bf16)
        if r % 2 == 1:
            ready = pl.ds(r - 1, 2)
            copies.append(
                pltpu.make_async_copy(staged.at[ready], sum_ref.at[ready], sems.at[r // 2])
            )
            copies[-1].start()
    for copy in copies:
        copy.wait()
    for copy in passing:
        copy.wait()


def project(count_ref, core_ref, tokens_ref, sums_ref, out_ref, held):
    ranks, planes, halves, rows, _ = sums_ref.shape
    for r in range(ranks):
        for h in range(halves):
            first = (2 * r + h) * 2 * rows
            total = sums_ref[r, 0, h].astype(f32)
            for y in range(1, planes):
                total = total + sums_ref[r, y, h].astype(f32)
            held[first : first + rows, :] = total.astype(bf16)
            held[first + rows : first + 2 * rows, :] = pltpu.roll(total, 64, 1).astype(bf16)
    full = jnp.dot(tokens_ref[...], held[...], preferred_element_type=f32).T
    mine = jnp.where(core_ref[0] == 0, full[:64], full[64:])
    live = lax.broadcasted_iota(jnp.int32, mine.shape, 1) < count_ref[0]
    out_ref[...] = jnp.where(live, mine * 8 ** (-0.5), 0.0).astype(bf16)


def body(grad, weight, owner, tokens, counts):
    number, rows, width = grad.shape
    ranks = lax.axis_size("row")
    planes = lax.axis_size("y")
    half = rows // 2
    index = lax.axis_index("core")
    core = index[None]
    vmem = pl.BlockSpec(memory_space=pltpu.VMEM)
    smem = pl.BlockSpec(memory_space=pltpu.SMEM)
    hbm = pl.BlockSpec(memory_space=pltpu.HBM)
    params = pltpu.CompilerParams(vmem_limit_bytes=20 * 1024 * 1024)
    swap = [(0, 1), (1, 0)]

    def exchange(data, axes):
        return lax.all_to_all(data, axes, split_axis=0, concat_axis=0, tiled=True)

    narrowed = pl.pallas_call(
        narrow,
        out_shape=jax.ShapeDtypeStruct(grad.shape, bf16),
        in_specs=[hbm],
        out_specs=vmem,
        scratch_shapes=[pltpu.VMEM(grad.shape, f32), pltpu.SemaphoreType.DMA((16,))],
        compiler_params=params,
        name="narrow",
    )(pltpu.with_memory_space_constraint(grad, pltpu.HBM))
    whole = exchange(narrowed, "row")

    named = owner[:, 0]
    mine, theirs, table = pl.pallas_call(
        gather_old,
        out_shape=(
            pltpu.HBM((ranks, half, width), bf16),
            pltpu.HBM((ranks, half, width), bf16),
            jax.ShapeDtypeStruct((2, number), jnp.int32),
        ),
        in_specs=[smem, smem, hbm],
        out_specs=(hbm, hbm, smem),
        scratch_shapes=[
            pltpu.VMEM((number, rows, width), bf16),
            pltpu.VMEM((2, ranks, half, width), bf16),
            pltpu.SemaphoreType.DMA((4,)),
            pltpu.SemaphoreType.DMA((2,)),
        ],
        compiler_params=params,
        name="gather_old",
    )(named, core, pltpu.with_memory_space_constraint(weight, pltpu.HBM))
    theirs = lax.ppermute(theirs, "core", swap)
    pair_table = lax.ppermute(table, "core", swap)
    old = (mine.astype(f32) + theirs.astype(f32)).astype(bf16)

    ortho = pl.pallas_call(
        orthogonalize,
        out_shape=pltpu.HBM((ranks * rows, width), bf16),
        in_specs=[vmem],
        out_specs=hbm,
        scratch_shapes=[
            pltpu.VMEM((width, width), bf16),
            pltpu.VMEM((ranks * rows, width), bf16),
            pltpu.VMEM((ranks * rows, width), bf16),
            pltpu.SemaphoreType.DMA((8,)),
        ],
        compiler_params=params,
        name="orthogonalize",
    )(whole.reshape(ranks * rows, width))
    back = exchange(ortho.reshape(2 * ranks, half, width), ("row", "core"))
    back = back.reshape(number, 2, half, width)

    lanes = half // 2
    sums, *passed = pl.pallas_call(
        combine,
        out_shape=(
            pltpu.HBM((ranks, 2 * planes, lanes, 128), bf16),
            *[pltpu.HBM((number // PIECES, half, width), bf16) for _ in range(PIECES)],
        ),
        in_specs=[smem, smem, smem, vmem, vmem],
        out_specs=(hbm,) * (1 + PIECES),
        scratch_shapes=[
            pltpu.VMEM((ranks, 2 * planes, lanes, 128), bf16),
            pltpu.SemaphoreType.DMA((8,)),
            pltpu.SemaphoreType.DMA((PIECES,)),
        ],
        compiler_params=params,
        name="combine",
    )(
        table,
        pair_table,
        core,
        old,
        back,
    )
    sums = exchange(sums.reshape(-1, lanes, 128), ("row", "y", "core"))
    sums = sums.reshape(ranks, planes, 2, lanes, 128)

    other = jnp.concatenate([lax.ppermute(piece, "core", swap) for piece in passed])
    own = lax.dynamic_index_in_dim(back, index, 1, keepdims=True)
    near = lax.broadcasted_iota(jnp.int32, (1, 2, 1, 1), 1) == index
    move = jnp.where(near, own, other[:, None])
    new = weight.reshape(move.shape).astype(f32) - step_size * move.astype(f32)
    new = new.astype(bf16).reshape(weight.shape)
    new, sums = lax.optimization_barrier((new, sums))
    mixed = pl.pallas_call(
        project,
        out_shape=jax.ShapeDtypeStruct((width // (2 * planes), tokens.shape[0]), bf16),
        in_specs=[smem, smem, vmem, vmem],
        out_specs=vmem,
        scratch_shapes=[pltpu.VMEM((ranks * rows, 128), bf16)],
        compiler_params=params,
        name="project",
    )(counts, core, tokens, sums)
    return new, mixed.T


def solution(mesh):
    devices = mesh.devices.reshape(mesh.shape["grp"] // 2, 2, mesh.shape["row"])
    inner = Mesh(devices, ("y", "core", "row"))
    group = ("y", "core")
    return jax.shard_map(
        body,
        mesh=inner,
        in_specs=(
            P(group, "row", None),
            P(group, "row", None),
            P(group, None),
            P("row", None),
            P("row"),
        ),
        out_specs=(P(group, "row", None), P("row", group)),
        check_vma=False,
    )
```

```python
import jax
import jax.numpy as jnp
from jax import lax
from jax.experimental import pallas as pl
from jax.experimental.pallas import tpu as pltpu
from jax.sharding import Mesh
from jax.sharding import PartitionSpec as P

ITERS = 5
coef_a = 3.4445
coef_b = -4.775
coef_c = 2.0315
step_size = 0.5
PIECES = 2

f32 = jnp.float32
bf16 = jnp.bfloat16


def narrow(far_ref, out_ref, held, sems):
    parts = sems.shape[0]
    size = out_ref.shape[0] // parts
    copies = []
    for part in range(parts):
        some = pl.ds(part * size, size)
        copies.append(pltpu.make_async_copy(far_ref.at[some], held.at[some], sems.at[part]))
        copies[-1].start()
    for part in range(parts):
        copies[part].wait()
        some = pl.ds(part * size, size)
        out_ref[some] = held[some].astype(bf16)


def cross(left, right):
    return lax.dot_general(left, right, (((0,), (0,)), ((), ())), preferred_element_type=f32)


def trace(block):
    diagonal = lax.broadcasted_iota(jnp.int32, block.shape, 0) == lax.broadcasted_iota(
        jnp.int32, block.shape, 1
    )
    total = jnp.sum(jnp.where(diagonal, block, 0.0), axis=0, keepdims=True)
    return jnp.sum(total, axis=1, keepdims=True)


def orthogonalize(x_ref, out_ref, gram_ref, held, staged, sems):
    rows, width = x_ref.shape
    low, high = slice(0, width // 2), slice(width // 2, width)
    copies = []
    scale = None
    for turn in range(ITERS):
        source = x_ref if turn == 0 else held
        left, right = source[:, low], source[:, high]
        upper = cross(left, right)
        if turn == 0:
            first, last = cross(left, left), cross(right, right)
            norm2 = trace(first) + trace(last)
            scale = 1.0 / (jnp.sqrt(norm2) + 1e-07)

            def scaled(block):
                return jnp.where(norm2 < jnp.inf, block * scale * scale, 0.0)

            upper, first, last = scaled(upper), scaled(first), scaled(last)
        gram_ref[low, high] = upper.astype(bf16)
        gram_ref[high, low] = upper.T.astype(bf16)
        gram_ref[low, low] = (first if turn == 0 else cross(left, left)).astype(bf16)
        gram_ref[high, high] = (last if turn == 0 else cross(right, right)).astype(bf16)
        g = gram_ref[...]
        square = jnp.dot(g, g, preferred_element_type=f32)
        poly = (coef_b * g.astype(f32) + coef_c * square).astype(bf16)
        parts = 4 if turn < ITERS - 1 else sems.shape[0]
        step = rows // parts
        for part in range(parts):
            at = pl.ds(part * step, step)
            piece = source[at, :]
            fresh = coef_a * piece.astype(f32) + jnp.dot(piece, poly, preferred_element_type=f32)
            if turn == 0:
                fresh = fresh * scale
            fresh = fresh.astype(bf16)
            if turn < ITERS - 1:
                held[at, :] = fresh
                continue
            staged[at, :] = fresh
            copies.append(pltpu.make_async_copy(staged.at[at], out_ref.at[at], sems.at[part]))
            copies[-1].start()
    for copy in copies:
        copy.wait()


def list_owned(named, table):
    for r in range(named.shape[0]):
        table[0, r] = -1
        table[1, r] = -1
    for e in range(named.shape[0]):
        o = named[e]
        seen = table[0, o] >= 0
        table[1, o] = jnp.where(seen, e, table[1, o])
        table[0, o] = jnp.where(seen, table[0, o], e)


def gather_old(owner_ref, core_ref, weight_ref, keep_ref, send_ref, table, held, staged, *sems):
    in_sems, out_sems = sems
    number, rows, width = weight_ref.shape
    half = rows // 2
    core = core_ref[0]
    arriving = []
    for part in range(4):
        some = pl.ds(part * (number // 4), number // 4)
        arriving.append(
            pltpu.make_async_copy(weight_ref.at[some], held.at[some], in_sems.at[part])
        )
        arriving[-1].start()
    list_owned(owner_ref, table)
    for copy in arriving:
        copy.wait()
    copies = []
    for place, out_ref in enumerate((send_ref, keep_ref)):
        near = core if place else 1 - core
        at = pl.ds(pl.multiple_of(near * half, half), half)
        for r in range(number):
            total = 0.0
            for slot in range(2):
                e = table[slot, r]
                old = held[jnp.maximum(e, 0), at, :].astype(f32)
                total = total + jnp.where(e >= 0, old, 0.0)
            staged[place, r] = total.astype(bf16)
        copies.append(pltpu.make_async_copy(staged.at[place], out_ref, out_sems.at[place]))
        copies[-1].start()
    for copy in copies:
        copy.wait()


def combine(table_ref, pair_ref, core_ref, old_ref, ortho_ref, *refs):
    sum_ref, pass_refs, (staged, sems, pass_sems) = refs[0], refs[1:-3], refs[-3:]
    number, halves, rows, width = ortho_ref.shape
    lanes = rows // 2
    tiles = width // 128
    core = core_ref[0]
    passing = []
    for part, pass_ref in enumerate(pass_refs):
        some = pl.ds(part * pass_ref.shape[0], pass_ref.shape[0])
        passing.append(
            pltpu.make_async_copy(ortho_ref.at[some, 1 - core], pass_ref, pass_sems.at[part])
        )
        passing[-1].start()
    low = lax.broadcasted_iota(jnp.int32, (lanes, 128), 1) < 64
    copies = []
    for r in range(number):
        slots = []
        for slot in range(4):
            e = (table_ref if slot < 2 else pair_ref)[slot % 2, r]
            source = core if slot < 2 else 1 - core
            slots.append((e >= 0, jnp.maximum(e, 0), source))
        for t in range(tiles):
            columns = slice(t * 128, (t + 1) * 128)
            move = 0.0
            for listed, at, source in slots:
                one = ortho_ref[at, source, :, columns].astype(f32)
                move = move + jnp.where(listed, one, 0.0)
            total = old_ref[r, :, columns].astype(f32) - step_size * move
            top = total[:lanes]
            bottom = pltpu.roll(total[lanes:], 64, 1)
            staged[r, 2 * t] = jnp.where(low, top, bottom).astype(bf16)
            staged[r, 2 * t + 1] = jnp.where(low, bottom, top).astype(bf16)
        if r % 2 == 1:
            ready = pl.ds(r - 1, 2)
            copies.append(
                pltpu.make_async_copy(staged.at[ready], sum_ref.at[ready], sems.at[r // 2])
            )
            copies[-1].start()
    for copy in copies:
        copy.wait()
    for copy in passing:
        copy.wait()


def project(count_ref, core_ref, tokens_ref, sums_ref, out_ref, held):
    ranks, planes, halves, rows, _ = sums_ref.shape
    for r in range(ranks):
        for h in range(halves):
            first = (2 * r + h) * 2 * rows
            total = sums_ref[r, 0, h].astype(f32)
            for y in range(1, planes):
                total = total + sums_ref[r, y, h].astype(f32)
            held[first : first + rows, :] = total.astype(bf16)
            held[first + rows : first + 2 * rows, :] = pltpu.roll(total, 64, 1).astype(bf16)
    full = jnp.dot(tokens_ref[...], held[...], preferred_element_type=f32).T
    mine = jnp.where(core_ref[0] == 0, full[:64], full[64:])
    live = lax.broadcasted_iota(jnp.int32, mine.shape, 1) < count_ref[0]
    out_ref[...] = jnp.where(live, mine * 8 ** (-0.5), 0.0).astype(bf16)


def body(grad, weight, owner, tokens, counts):
    number, rows, width = grad.shape
    ranks = lax.axis_size("z") * lax.axis_size("x")
    planes = lax.axis_size("y")
    half = rows // 2
    index = lax.axis_index("core")
    core = index[None]
    vmem = pl.BlockSpec(memory_space=pltpu.VMEM)
    smem = pl.BlockSpec(memory_space=pltpu.SMEM)
    hbm = pl.BlockSpec(memory_space=pltpu.HBM)
    params = pltpu.CompilerParams(vmem_limit_bytes=20 * 1024 * 1024)
    swap = [(0, 1), (1, 0)]

    def exchange(data, axes):
        return lax.all_to_all(data, axes, split_axis=0, concat_axis=0, tiled=True)

    narrowed = pl.pallas_call(
        narrow,
        out_shape=jax.ShapeDtypeStruct(grad.shape, bf16),
        in_specs=[hbm],
        out_specs=vmem,
        scratch_shapes=[pltpu.VMEM(grad.shape, f32), pltpu.SemaphoreType.DMA((16,))],
        compiler_params=params,
        name="narrow",
    )(pltpu.with_memory_space_constraint(grad, pltpu.HBM))
    whole = exchange(narrowed, ("x", "z"))

    named = owner[:, 0]
    mine, theirs, table = pl.pallas_call(
        gather_old,
        out_shape=(
            pltpu.HBM((ranks, half, width), bf16),
            pltpu.HBM((ranks, half, width), bf16),
            jax.ShapeDtypeStruct((2, number), jnp.int32),
        ),
        in_specs=[smem, smem, hbm],
        out_specs=(hbm, hbm, smem),
        scratch_shapes=[
            pltpu.VMEM((number, rows, width), bf16),
            pltpu.VMEM((2, ranks, half, width), bf16),
            pltpu.SemaphoreType.DMA((4,)),
            pltpu.SemaphoreType.DMA((2,)),
        ],
        compiler_params=params,
        name="gather_old",
    )(named, core, pltpu.with_memory_space_constraint(weight, pltpu.HBM))
    theirs = lax.ppermute(theirs, "core", swap)
    pair_table = lax.ppermute(table, "core", swap)
    old = (mine.astype(f32) + theirs.astype(f32)).astype(bf16)

    ortho = pl.pallas_call(
        orthogonalize,
        out_shape=pltpu.HBM((ranks * rows, width), bf16),
        in_specs=[vmem],
        out_specs=hbm,
        scratch_shapes=[
            pltpu.VMEM((width, width), bf16),
            pltpu.VMEM((ranks * rows, width), bf16),
            pltpu.VMEM((ranks * rows, width), bf16),
            pltpu.SemaphoreType.DMA((8,)),
        ],
        compiler_params=params,
        name="orthogonalize",
    )(whole.reshape(ranks * rows, width))
    back = exchange(ortho.reshape(2 * ranks, half, width), ("x", "z", "core"))
    back = back.reshape(number, 2, half, width)

    lanes = half // 2
    sums, *passed = pl.pallas_call(
        combine,
        out_shape=(
            pltpu.HBM((ranks, 2 * planes, lanes, 128), bf16),
            *[pltpu.HBM((number // PIECES, half, width), bf16) for _ in range(PIECES)],
        ),
        in_specs=[smem, smem, smem, vmem, vmem],
        out_specs=(hbm,) * (1 + PIECES),
        scratch_shapes=[
            pltpu.VMEM((ranks, 2 * planes, lanes, 128), bf16),
            pltpu.SemaphoreType.DMA((8,)),
            pltpu.SemaphoreType.DMA((PIECES,)),
        ],
        compiler_params=params,
        name="combine",
    )(
        table,
        pair_table,
        core,
        old,
        back,
    )
    sums = exchange(sums.reshape(-1, lanes, 128), ("z", "x", "y", "core"))
    sums = sums.reshape(ranks, planes, 2, lanes, 128)

    other = jnp.concatenate([lax.ppermute(piece, "core", swap) for piece in passed])
    own = lax.dynamic_index_in_dim(back, index, 1, keepdims=True)
    near = lax.broadcasted_iota(jnp.int32, (1, 2, 1, 1), 1) == index
    move = jnp.where(near, own, other[:, None])
    new = weight.reshape(move.shape).astype(f32) - step_size * move.astype(f32)
    new = new.astype(bf16).reshape(weight.shape)
    new, sums = lax.optimization_barrier((new, sums))
    mixed = pl.pallas_call(
        project,
        out_shape=jax.ShapeDtypeStruct((width // (2 * planes), tokens.shape[0]), bf16),
        in_specs=[smem, smem, vmem, vmem],
        out_specs=vmem,
        scratch_shapes=[pltpu.VMEM((ranks * rows, 128), bf16)],
        compiler_params=params,
        name="project",
    )(counts, core, tokens, sums)
    return new, mixed.T


def solution(mesh):
    side = round(mesh.shape["row"] ** 0.5)
    devices = mesh.devices.reshape(mesh.shape["grp"] // 2, 2, side, side)
    inner = Mesh(devices, ("y", "core", "z", "x"))
    group, row = ("y", "core"), ("z", "x")
    return jax.shard_map(
        body,
        mesh=inner,
        in_specs=(
            P(group, row, None),
            P(group, row, None),
            P(group, None),
            P(row, None),
            P(row),
        ),
        out_specs=(P(group, row, None), P(row, group)),
        check_vma=False,
    )
```

```python
import jax
import jax.numpy as jnp
from jax import lax
from jax.experimental import pallas as pl
from jax.experimental.pallas import tpu as pltpu
from jax.sharding import Mesh
from jax.sharding import PartitionSpec as P

ITERS = 5
coef_a = 3.4445
coef_b = -4.775
coef_c = 2.0315
step_size = 0.5
PIECES = 2

f32 = jnp.float32
bf16 = jnp.bfloat16


def narrow(far_ref, out_ref, held, sems):
    parts = sems.shape[0]
    size = out_ref.shape[0] // parts
    copies = []
    for part in range(parts):
        some = pl.ds(part * size, size)
        copies.append(pltpu.make_async_copy(far_ref.at[some], held.at[some], sems.at[part]))
        copies[-1].start()
    for part in range(parts):
        copies[part].wait()
        some = pl.ds(part * size, size)
        out_ref[some] = held[some].astype(bf16)


def cross(left, right):
    return lax.dot_general(left, right, (((0,), (0,)), ((), ())), preferred_element_type=f32)


def trace(block):
    diagonal = lax.broadcasted_iota(jnp.int32, block.shape, 0) == lax.broadcasted_iota(
        jnp.int32, block.shape, 1
    )
    total = jnp.sum(jnp.where(diagonal, block, 0.0), axis=0, keepdims=True)
    return jnp.sum(total, axis=1, keepdims=True)


def orthogonalize(x_ref, out_ref, gram_ref, held, staged, sems):
    rows, width = x_ref.shape
    low, high = slice(0, width // 2), slice(width // 2, width)
    copies = []
    scale = None
    for turn in range(ITERS):
        source = x_ref if turn == 0 else held
        left, right = source[:, low], source[:, high]
        upper = cross(left, right)
        if turn == 0:
            first, last = cross(left, left), cross(right, right)
            norm2 = trace(first) + trace(last)
            scale = 1.0 / (jnp.sqrt(norm2) + 1e-07)

            def scaled(block):
                return jnp.where(norm2 < jnp.inf, block * scale * scale, 0.0)

            upper, first, last = scaled(upper), scaled(first), scaled(last)
        gram_ref[low, high] = upper.astype(bf16)
        gram_ref[high, low] = upper.T.astype(bf16)
        gram_ref[low, low] = (first if turn == 0 else cross(left, left)).astype(bf16)
        gram_ref[high, high] = (last if turn == 0 else cross(right, right)).astype(bf16)
        g = gram_ref[...]
        square = jnp.dot(g, g, preferred_element_type=f32)
        poly = (coef_b * g.astype(f32) + coef_c * square).astype(bf16)
        parts = 4 if turn < ITERS - 1 else sems.shape[0]
        step = rows // parts
        for part in range(parts):
            at = pl.ds(part * step, step)
            piece = source[at, :]
            fresh = coef_a * piece.astype(f32) + jnp.dot(piece, poly, preferred_element_type=f32)
            if turn == 0:
                fresh = fresh * scale
            fresh = fresh.astype(bf16)
            if turn < ITERS - 1:
                held[at, :] = fresh
                continue
            staged[at, :] = fresh
            copies.append(pltpu.make_async_copy(staged.at[at], out_ref.at[at], sems.at[part]))
            copies[-1].start()
    for copy in copies:
        copy.wait()


def list_owned(named, table):
    for r in range(named.shape[0]):
        table[0, r] = -1
        table[1, r] = -1
    for e in range(named.shape[0]):
        o = named[e]
        seen = table[0, o] >= 0
        table[1, o] = jnp.where(seen, e, table[1, o])
        table[0, o] = jnp.where(seen, table[0, o], e)


def gather_old(owner_ref, core_ref, weight_ref, keep_ref, send_ref, table, held, staged, *sems):
    in_sems, out_sems = sems
    number, rows, width = weight_ref.shape
    half = rows // 2
    core = core_ref[0]
    arriving = []
    for part in range(4):
        some = pl.ds(part * (number // 4), number // 4)
        arriving.append(
            pltpu.make_async_copy(weight_ref.at[some], held.at[some], in_sems.at[part])
        )
        arriving[-1].start()
    list_owned(owner_ref, table)
    for copy in arriving:
        copy.wait()
    copies = []
    for place, out_ref in enumerate((send_ref, keep_ref)):
        near = core if place else 1 - core
        at = pl.ds(pl.multiple_of(near * half, half), half)
        for r in range(number):
            total = 0.0
            for slot in range(2):
                e = table[slot, r]
                old = held[jnp.maximum(e, 0), at, :].astype(f32)
                total = total + jnp.where(e >= 0, old, 0.0)
            staged[place, r] = total.astype(bf16)
        copies.append(pltpu.make_async_copy(staged.at[place], out_ref, out_sems.at[place]))
        copies[-1].start()
    for copy in copies:
        copy.wait()


def combine(table_ref, pair_ref, core_ref, old_ref, ortho_ref, *refs):
    sum_ref, pass_refs, (staged, sems, pass_sems) = refs[0], refs[1:-3], refs[-3:]
    number, halves, rows, width = ortho_ref.shape
    lanes = rows // 2
    tiles = width // 128
    core = core_ref[0]
    passing = []
    for part, pass_ref in enumerate(pass_refs):
        some = pl.ds(part * pass_ref.shape[0], pass_ref.shape[0])
        passing.append(
            pltpu.make_async_copy(ortho_ref.at[some, 1 - core], pass_ref, pass_sems.at[part])
        )
        passing[-1].start()
    low = lax.broadcasted_iota(jnp.int32, (lanes, 128), 1) < 64
    copies = []
    for k in range(number):
        r = k % 4 * 4 + k // 4
        slots = []
        for slot in range(4):
            e = (table_ref if slot < 2 else pair_ref)[slot % 2, r]
            source = core if slot < 2 else 1 - core
            slots.append((e >= 0, jnp.maximum(e, 0), source))
        for t in range(tiles):
            columns = slice(t * 128, (t + 1) * 128)
            move = 0.0
            for listed, at, source in slots:
                one = ortho_ref[at, source, :, columns].astype(f32)
                move = move + jnp.where(listed, one, 0.0)
            total = old_ref[r, :, columns].astype(f32) - step_size * move
            top = total[:lanes]
            bottom = pltpu.roll(total[lanes:], 64, 1)
            staged[k, 2 * t] = jnp.where(low, top, bottom).astype(bf16)
            staged[k, 2 * t + 1] = jnp.where(low, bottom, top).astype(bf16)
        if k % 2 == 1:
            ready = pl.ds(k - 1, 2)
            copies.append(
                pltpu.make_async_copy(staged.at[ready], sum_ref.at[ready], sems.at[k // 2])
            )
            copies[-1].start()
    for copy in copies:
        copy.wait()
    for copy in passing:
        copy.wait()


def project(count_ref, core_ref, tokens_ref, sums_ref, out_ref, held):
    ranks, planes, halves, rows, _ = sums_ref.shape
    for k in range(ranks):
        r = k % 4 * 4 + k // 4
        for h in range(halves):
            first = (2 * r + h) * 2 * rows
            total = sums_ref[k, 0, h].astype(f32)
            for y in range(1, planes):
                total = total + sums_ref[k, y, h].astype(f32)
            held[first : first + rows, :] = total.astype(bf16)
            held[first + rows : first + 2 * rows, :] = pltpu.roll(total, 64, 1).astype(bf16)
    full = jnp.dot(tokens_ref[...], held[...], preferred_element_type=f32).T
    mine = jnp.where(core_ref[0] == 0, full[:64], full[64:])
    live = lax.broadcasted_iota(jnp.int32, mine.shape, 1) < count_ref[0]
    out_ref[...] = jnp.where(live, mine * 8 ** (-0.5), 0.0).astype(bf16)


def body(grad, weight, owner, tokens, counts):
    number, rows, width = grad.shape
    ranks = lax.axis_size("z") * lax.axis_size("x")
    planes = lax.axis_size("y")
    half = rows // 2
    index = lax.axis_index("core")
    core = index[None]
    vmem = pl.BlockSpec(memory_space=pltpu.VMEM)
    smem = pl.BlockSpec(memory_space=pltpu.SMEM)
    hbm = pl.BlockSpec(memory_space=pltpu.HBM)
    params = pltpu.CompilerParams(vmem_limit_bytes=20 * 1024 * 1024)
    swap = [(0, 1), (1, 0)]

    def exchange(data, axes):
        return lax.all_to_all(data, axes, split_axis=0, concat_axis=0, tiled=True)

    narrowed = pl.pallas_call(
        narrow,
        out_shape=jax.ShapeDtypeStruct(grad.shape, bf16),
        in_specs=[hbm],
        out_specs=vmem,
        scratch_shapes=[pltpu.VMEM(grad.shape, f32), pltpu.SemaphoreType.DMA((16,))],
        compiler_params=params,
        name="narrow",
    )(pltpu.with_memory_space_constraint(grad, pltpu.HBM))
    whole = exchange(narrowed, ("x", "z"))

    named = owner[:, 0]
    mine, theirs, table = pl.pallas_call(
        gather_old,
        out_shape=(
            pltpu.HBM((ranks, half, width), bf16),
            pltpu.HBM((ranks, half, width), bf16),
            jax.ShapeDtypeStruct((2, number), jnp.int32),
        ),
        in_specs=[smem, smem, hbm],
        out_specs=(hbm, hbm, smem),
        scratch_shapes=[
            pltpu.VMEM((number, rows, width), bf16),
            pltpu.VMEM((2, ranks, half, width), bf16),
            pltpu.SemaphoreType.DMA((4,)),
            pltpu.SemaphoreType.DMA((2,)),
        ],
        compiler_params=params,
        name="gather_old",
    )(named, core, pltpu.with_memory_space_constraint(weight, pltpu.HBM))
    theirs = lax.ppermute(theirs, "core", swap)
    pair_table = lax.ppermute(table, "core", swap)
    old = (mine.astype(f32) + theirs.astype(f32)).astype(bf16)

    ortho = pl.pallas_call(
        orthogonalize,
        out_shape=pltpu.HBM((ranks * rows, width), bf16),
        in_specs=[vmem],
        out_specs=hbm,
        scratch_shapes=[
            pltpu.VMEM((width, width), bf16),
            pltpu.VMEM((ranks * rows, width), bf16),
            pltpu.VMEM((ranks * rows, width), bf16),
            pltpu.SemaphoreType.DMA((8,)),
        ],
        compiler_params=params,
        name="orthogonalize",
    )(whole.reshape(ranks * rows, width))
    back = exchange(ortho.reshape(2 * ranks, half, width), ("x", "z", "core"))
    back = back.reshape(number, 2, half, width)

    lanes = half // 2
    sums, *passed = pl.pallas_call(
        combine,
        out_shape=(
            pltpu.HBM((ranks, 2 * planes, lanes, 128), bf16),
            *[pltpu.HBM((number // PIECES, half, width), bf16) for _ in range(PIECES)],
        ),
        in_specs=[smem, smem, smem, vmem, vmem],
        out_specs=(hbm,) * (1 + PIECES),
        scratch_shapes=[
            pltpu.VMEM((ranks, 2 * planes, lanes, 128), bf16),
            pltpu.SemaphoreType.DMA((8,)),
            pltpu.SemaphoreType.DMA((PIECES,)),
        ],
        compiler_params=params,
        name="combine",
    )(
        table,
        pair_table,
        core,
        old,
        back,
    )
    sums = exchange(sums.reshape(-1, lanes, 128), ("x", "z", "y", "core"))
    sums = sums.reshape(ranks, planes, 2, lanes, 128)

    other = jnp.concatenate([lax.ppermute(piece, "core", swap) for piece in passed])
    own = lax.dynamic_index_in_dim(back, index, 1, keepdims=True)
    near = lax.broadcasted_iota(jnp.int32, (1, 2, 1, 1), 1) == index
    move = jnp.where(near, own, other[:, None])
    new = weight.reshape(move.shape).astype(f32) - step_size * move.astype(f32)
    new = new.astype(bf16).reshape(weight.shape)
    new, sums = lax.optimization_barrier((new, sums))
    mixed = pl.pallas_call(
        project,
        out_shape=jax.ShapeDtypeStruct((width // (2 * planes), tokens.shape[0]), bf16),
        in_specs=[smem, smem, vmem, vmem],
        out_specs=vmem,
        scratch_shapes=[pltpu.VMEM((ranks * rows, 128), bf16)],
        compiler_params=params,
        name="project",
    )(counts, core, tokens, sums)
    return new, mixed.T


def solution(mesh):
    side = round(mesh.shape["row"] ** 0.5)
    devices = mesh.devices.reshape(mesh.shape["grp"] // 2, 2, side, side)
    inner = Mesh(devices, ("y", "core", "z", "x"))
    group, row = ("y", "core"), ("z", "x")
    return jax.shard_map(
        body,
        mesh=inner,
        in_specs=(
            P(group, row, None),
            P(group, row, None),
            P(group, None),
            P(row, None),
            P(row),
        ),
        out_specs=(P(group, row, None), P(row, group)),
        check_vma=False,
    )
```

```python
import jax
import jax.numpy as jnp
from jax import lax
from jax.experimental import pallas as pl
from jax.experimental.pallas import tpu as pltpu
from jax.sharding import Mesh
from jax.sharding import PartitionSpec as P

ITERS = 5
coef_a = 3.4445
coef_b = -4.775
coef_c = 2.0315
step_size = 0.5
PIECES = 2

f32 = jnp.float32
bf16 = jnp.bfloat16


def narrow(far_ref, out_ref, held, sems):
    parts = sems.shape[0]
    size = out_ref.shape[0] // parts
    copies = []
    for part in range(parts):
        some = pl.ds(part * size, size)
        copies.append(pltpu.make_async_copy(far_ref.at[some], held.at[some], sems.at[part]))
        copies[-1].start()
    for part in range(parts):
        copies[part].wait()
        some = pl.ds(part * size, size)
        out_ref[some] = held[some].astype(bf16)


def cross(left, right):
    return lax.dot_general(left, right, (((0,), (0,)), ((), ())), preferred_element_type=f32)


def trace(block):
    diagonal = lax.broadcasted_iota(jnp.int32, block.shape, 0) == lax.broadcasted_iota(
        jnp.int32, block.shape, 1
    )
    total = jnp.sum(jnp.where(diagonal, block, 0.0), axis=0, keepdims=True)
    return jnp.sum(total, axis=1, keepdims=True)


def orthogonalize(x_ref, out_ref, gram_ref, held, staged, sems):
    rows, width = x_ref.shape
    low, high = slice(0, width // 2), slice(width // 2, width)
    copies = []
    scale = None
    for turn in range(ITERS):
        source = x_ref if turn == 0 else held
        left, right = source[:, low], source[:, high]
        upper = cross(left, right)
        if turn == 0:
            first, last = cross(left, left), cross(right, right)
            norm2 = trace(first) + trace(last)
            scale = 1.0 / (jnp.sqrt(norm2) + 1e-07)

            def scaled(block):
                return jnp.where(norm2 < jnp.inf, block * scale * scale, 0.0)

            upper, first, last = scaled(upper), scaled(first), scaled(last)
        gram_ref[low, high] = upper.astype(bf16)
        gram_ref[high, low] = upper.T.astype(bf16)
        gram_ref[low, low] = (first if turn == 0 else cross(left, left)).astype(bf16)
        gram_ref[high, high] = (last if turn == 0 else cross(right, right)).astype(bf16)
        g = gram_ref[...]
        square = jnp.dot(g, g, preferred_element_type=f32)
        poly = (coef_b * g.astype(f32) + coef_c * square).astype(bf16)
        parts = 4 if turn < ITERS - 1 else sems.shape[0]
        step = rows // parts
        for part in range(parts):
            at = pl.ds(part * step, step)
            piece = source[at, :]
            fresh = coef_a * piece.astype(f32) + jnp.dot(piece, poly, preferred_element_type=f32)
            if turn == 0:
                fresh = fresh * scale
            fresh = fresh.astype(bf16)
            if turn < ITERS - 1:
                held[at, :] = fresh
                continue
            staged[at, :] = fresh
            copies.append(pltpu.make_async_copy(staged.at[at], out_ref.at[at], sems.at[part]))
            copies[-1].start()
    for copy in copies:
        copy.wait()


def list_owned(named, table):
    for r in range(named.shape[0]):
        table[0, r] = -1
        table[1, r] = -1
    for e in range(named.shape[0]):
        o = named[e]
        seen = table[0, o] >= 0
        table[1, o] = jnp.where(seen, e, table[1, o])
        table[0, o] = jnp.where(seen, table[0, o], e)


def gather_old(owner_ref, core_ref, weight_ref, keep_ref, send_ref, table, held, staged, *sems):
    in_sems, out_sems = sems
    number, rows, width = weight_ref.shape
    half = rows // 2
    core = core_ref[0]
    arriving = []
    for part in range(4):
        some = pl.ds(part * (number // 4), number // 4)
        arriving.append(
            pltpu.make_async_copy(weight_ref.at[some], held.at[some], in_sems.at[part])
        )
        arriving[-1].start()
    list_owned(owner_ref, table)
    for copy in arriving:
        copy.wait()
    copies = []
    for place, out_ref in enumerate((send_ref, keep_ref)):
        near = core if place else 1 - core
        at = pl.ds(pl.multiple_of(near * half, half), half)
        for r in range(number):
            total = 0.0
            for slot in range(2):
                e = table[slot, r]
                old = held[jnp.maximum(e, 0), at, :].astype(f32)
                total = total + jnp.where(e >= 0, old, 0.0)
            staged[place, r] = total.astype(bf16)
        copies.append(pltpu.make_async_copy(staged.at[place], out_ref, out_sems.at[place]))
        copies[-1].start()
    for copy in copies:
        copy.wait()


def combine(table_ref, pair_ref, core_ref, old_ref, ortho_ref, *refs):
    sum_ref, pass_refs, (staged, sems, pass_sems) = refs[0], refs[1:-3], refs[-3:]
    number, halves, rows, width = ortho_ref.shape
    lanes = rows // 2
    tiles = width // 128
    core = core_ref[0]
    passing = []
    for part, pass_ref in enumerate(pass_refs):
        some = pl.ds(part * pass_ref.shape[0], pass_ref.shape[0])
        passing.append(
            pltpu.make_async_copy(ortho_ref.at[some, 1 - core], pass_ref, pass_sems.at[part])
        )
        passing[-1].start()
    low = lax.broadcasted_iota(jnp.int32, (lanes, 128), 1) < 64
    copies = []
    for k in range(number):
        r = k % 4 * 4 + k // 4
        slots = []
        for slot in range(4):
            e = (table_ref if slot < 2 else pair_ref)[slot % 2, r]
            source = core if slot < 2 else 1 - core
            slots.append((e >= 0, jnp.maximum(e, 0), source))
        for t in range(tiles):
            columns = slice(t * 128, (t + 1) * 128)
            move = 0.0
            for listed, at, source in slots:
                one = ortho_ref[at, source, :, columns].astype(f32)
                move = move + jnp.where(listed, one, 0.0)
            total = old_ref[r, :, columns].astype(f32) - step_size * move
            top = total[:lanes]
            bottom = pltpu.roll(total[lanes:], 64, 1)
            staged[k, 2 * t] = jnp.where(low, top, bottom).astype(bf16)
            staged[k, 2 * t + 1] = jnp.where(low, bottom, top).astype(bf16)
        if k % 2 == 1:
            ready = pl.ds(k - 1, 2)
            copies.append(
                pltpu.make_async_copy(staged.at[ready], sum_ref.at[ready], sems.at[k // 2])
            )
            copies[-1].start()
    for copy in copies:
        copy.wait()
    for copy in passing:
        copy.wait()


def project(count_ref, core_ref, tokens_ref, sums_ref, out_ref, held):
    ranks, planes, halves, rows, _ = sums_ref.shape
    for k in range(ranks):
        r = k % 4 * 4 + k // 4
        for h in range(halves):
            first = (2 * r + h) * 2 * rows
            total = sums_ref[k, 0, h].astype(f32)
            for y in range(1, planes):
                total = total + sums_ref[k, y, h].astype(f32)
            held[first : first + rows, :] = total.astype(bf16)
            held[first + rows : first + 2 * rows, :] = pltpu.roll(total, 64, 1).astype(bf16)
    full = jnp.dot(tokens_ref[...], held[...], preferred_element_type=f32).T
    mine = jnp.where(core_ref[0] == 0, full[:64], full[64:])
    live = lax.broadcasted_iota(jnp.int32, mine.shape, 1) < count_ref[0]
    out_ref[...] = jnp.where(live, mine * 8 ** (-0.5), 0.0).astype(bf16)


def body(grad, weight, owner, tokens, counts):
    number, rows, width = grad.shape
    ranks = lax.axis_size("z") * lax.axis_size("x")
    planes = lax.axis_size("y")
    half = rows // 2
    index = lax.axis_index("core")
    core = index[None]
    vmem = pl.BlockSpec(memory_space=pltpu.VMEM)
    smem = pl.BlockSpec(memory_space=pltpu.SMEM)
    hbm = pl.BlockSpec(memory_space=pltpu.HBM)
    params = pltpu.CompilerParams(vmem_limit_bytes=20 * 1024 * 1024)
    swap = [(0, 1), (1, 0)]

    def exchange(data, axes):
        return lax.all_to_all(data, axes, split_axis=0, concat_axis=0, tiled=True)

    narrowed = pl.pallas_call(
        narrow,
        out_shape=jax.ShapeDtypeStruct(grad.shape, bf16),
        in_specs=[hbm],
        out_specs=vmem,
        scratch_shapes=[pltpu.VMEM(grad.shape, f32), pltpu.SemaphoreType.DMA((8,))],
        compiler_params=params,
        name="narrow",
    )(pltpu.with_memory_space_constraint(grad, pltpu.HBM))
    whole = exchange(narrowed, ("x", "z"))

    named = owner[:, 0]
    mine, theirs, table = pl.pallas_call(
        gather_old,
        out_shape=(
            pltpu.HBM((ranks, half, width), bf16),
            pltpu.HBM((ranks, half, width), bf16),
            jax.ShapeDtypeStruct((2, number), jnp.int32),
        ),
        in_specs=[smem, smem, hbm],
        out_specs=(hbm, hbm, smem),
        scratch_shapes=[
            pltpu.VMEM((number, rows, width), bf16),
            pltpu.VMEM((2, ranks, half, width), bf16),
            pltpu.SemaphoreType.DMA((4,)),
            pltpu.SemaphoreType.DMA((2,)),
        ],
        compiler_params=params,
        name="gather_old",
    )(named, core, pltpu.with_memory_space_constraint(weight, pltpu.HBM))
    theirs = lax.ppermute(theirs, "core", swap)
    pair_table = lax.ppermute(table, "core", swap)
    old = (mine.astype(f32) + theirs.astype(f32)).astype(bf16)

    ortho = pl.pallas_call(
        orthogonalize,
        out_shape=pltpu.HBM((ranks * rows, width), bf16),
        in_specs=[vmem],
        out_specs=hbm,
        scratch_shapes=[
            pltpu.VMEM((width, width), bf16),
            pltpu.VMEM((ranks * rows, width), bf16),
            pltpu.VMEM((ranks * rows, width), bf16),
            pltpu.SemaphoreType.DMA((8,)),
        ],
        compiler_params=params,
        name="orthogonalize",
    )(whole.reshape(ranks * rows, width))
    back = exchange(ortho.reshape(2 * ranks, half, width), ("x", "z", "core"))
    back = back.reshape(number, 2, half, width)

    lanes = half // 2
    sums, *passed = pl.pallas_call(
        combine,
        out_shape=(
            pltpu.HBM((ranks, 2 * planes, lanes, 128), bf16),
            *[pltpu.HBM((number // PIECES, half, width), bf16) for _ in range(PIECES)],
        ),
        in_specs=[smem, smem, smem, vmem, vmem],
        out_specs=(hbm,) * (1 + PIECES),
        scratch_shapes=[
            pltpu.VMEM((ranks, 2 * planes, lanes, 128), bf16),
            pltpu.SemaphoreType.DMA((8,)),
            pltpu.SemaphoreType.DMA((PIECES,)),
        ],
        compiler_params=params,
        name="combine",
    )(
        table,
        pair_table,
        core,
        old,
        back,
    )
    sums = exchange(sums.reshape(-1, lanes, 128), ("x", "z", "y", "core"))
    sums = sums.reshape(ranks, planes, 2, lanes, 128)

    other = jnp.concatenate([lax.ppermute(piece, "core", swap) for piece in passed])
    own = lax.dynamic_index_in_dim(back, index, 1, keepdims=True)
    near = lax.broadcasted_iota(jnp.int32, (1, 2, 1, 1), 1) == index
    move = jnp.where(near, own, other[:, None])
    new = weight.reshape(move.shape).astype(f32) - step_size * move.astype(f32)
    new = new.astype(bf16).reshape(weight.shape)
    new, sums = lax.optimization_barrier((new, sums))
    mixed = pl.pallas_call(
        project,
        out_shape=jax.ShapeDtypeStruct((width // (2 * planes), tokens.shape[0]), bf16),
        in_specs=[smem, smem, vmem, vmem],
        out_specs=vmem,
        scratch_shapes=[pltpu.VMEM((ranks * rows, 128), bf16)],
        compiler_params=params,
        name="project",
    )(counts, core, tokens, sums)
    return new, mixed.T


def solution(mesh):
    side = round(mesh.shape["row"] ** 0.5)
    devices = mesh.devices.reshape(mesh.shape["grp"] // 2, 2, side, side)
    inner = Mesh(devices, ("y", "core", "z", "x"))
    group, row = ("y", "core"), ("z", "x")
    return jax.shard_map(
        body,
        mesh=inner,
        in_specs=(
            P(group, row, None),
            P(group, row, None),
            P(group, None),
            P(row, None),
            P(row),
        ),
        out_specs=(P(group, row, None), P(row, group)),
        check_vma=False,
    )
```
